32 devices in a mesh: groups: 2 (over y), rows: 8 (over z, core), cols: 2 (over x).
Axes of the slice: x: 2, y: 2, z: 4, core: 2. Of those that a mesh axis runs over, the one named last changes fastest.
Arguments:
- big_emb: bfloat16 [8192, 768], P(('groups', 'rows', 'cols')), parts along dimension 0, may hold values from -6 to 6
- big_order: int32 [8192], P(('groups', 'rows', 'cols')), parts along dimension 0, may hold values from 0 to 4095, each once
- small_emb: bfloat16 [32, 8, 16, 768], P(('groups', 'rows', 'cols')), parts along dimension 0, may hold values from -6 to 6
- small_clus: int32 [32, 8, 16], P(('groups', 'rows', 'cols')), parts along dimension 0, may hold values from -1 to 15, as said below
- small_order: int32 [32, 8, 16], P(('groups', 'rows', 'cols')), parts along dimension 0, may hold values from 0 to 2047, as said below
Outputs:
- big_best: float32 [8192], P(('groups', 'rows', 'cols')), parts along dimension 0
- small_best: float32 [32, 8, 16], P(('groups', 'rows', 'cols')), parts along dimension 0
The draws below stay inside these ranges and needn't reach their ends.
There are 2 independent parts, one for each index of `groups`. The reference program is written for one: setup_inputs(seed, part) draws one part's arguments, and reference() takes and returns one part's arrays. A program takes and returns all parts, laid end to end along the dimension named above; each array names one. Nothing has to cross between parts.
Inputs may be any that keep to these rules, and one draw needn't show every extreme that they name: `small_clus`: -1 marks an empty slot; otherwise one of the 16 clusters of the destination device. The slots to one destination from one source are at most 16 live, and in every draw some source fills all 16 slots to some destination. `small_order`: each value occurs once within each part within each part (each index of `groups`).
All inputs are finite; a program needn't handle non-finite values.
Results may differ from the reference program's by a relative error of at most 0.0012.
Values may be sent and summed in bfloat16 or wider, within the bound.
No kernel may reach another device: no remote copies, remote signals or barrier semaphores. Data moves between devices by JAX's collectives and lax.ppermute only.
A program may use at most 64 MiB of HBM per device.

```python
import jax
import jax.numpy as jnp
from jax import lax

D = 768
CAP = 16
KCL = 16
BIG = 4096
SRC = 16
N_ROWS = 8
N_COLS = 2


def draw_small_clus(key, part):
    base = jax.random.fold_in(key, 11)
    key_live, key_full, key_ids = jax.random.split(base, 3)
    pairs = N_ROWS * N_COLS * N_ROWS
    live = jax.random.randint(key_live, (pairs,), CAP // 3, CAP, dtype=jnp.int32)
    full_pair = jax.random.randint(key_full, (), 0, pairs, dtype=jnp.int32)
    live = jnp.where(jnp.arange(pairs, dtype=jnp.int32) == full_pair, CAP, live)
    ids = jax.random.randint(key_ids, (pairs, CAP), 0, KCL, dtype=jnp.int32)
    ids = ids.at[full_pair, 0].set(KCL - 1)
    slot_index = jnp.arange(CAP, dtype=jnp.int32)
    result = jnp.where(slot_index[None, :] < live[:, None], ids, -1)
    return result.reshape(N_ROWS * N_COLS, N_ROWS, CAP).astype(jnp.int32)


def draw_small_order(key, part):
    base = jax.random.fold_in(key, 23)
    total = N_ROWS * N_COLS * N_ROWS * CAP
    ranks = jax.random.permutation(base, jnp.arange(total, dtype=jnp.int32))
    return ranks.reshape(N_ROWS * N_COLS, N_ROWS, CAP).astype(jnp.int32)


def levels(rng, dims, cuts, smallest, high):
    factor_of = 1.0
    for axis_at, shards_of in cuts:
        draws = jax.random.uniform(jax.random.fold_in(jax.random.fold_in(rng, 6), axis_at), (shards_of,), jnp.float32, smallest / len(cuts), high / len(cuts))
        factor_of = factor_of * jnp.repeat(jnp.exp(draws), dims[axis_at] // shards_of).reshape((-1,) + (1,) * (len(dims) - 1 - axis_at))
    return factor_of


def centred(rng, shape, scale, bound, cuts=(), kind=jnp.bfloat16):
    array = jax.random.normal(rng, shape, jnp.float32) * scale
    if len(cuts) > 0:
        array = levels(rng, shape, cuts, -0.22, 0.18) * array
    return jnp.clip(array, min=-bound, max=bound).astype(kind)


def setup_inputs(seed: int = 0, part: int = 0) -> dict:
    streams_of = jax.random.split(jax.random.key(seed), 6)
    part_keys = jax.random.split(jax.random.fold_in(streams_of[5], part), 6)
    big_emb = centred(part_keys[0], (BIG, D), 1.0, 6.0, ((0, 16),))
    big_order = jax.random.permutation(part_keys[1], BIG).astype(jnp.int32)
    small_emb = centred(part_keys[2], (SRC, N_ROWS, CAP, D), 1.0, 6.0, ((0, 16),))
    small_clus = draw_small_clus(jax.random.fold_in(jax.random.fold_in(streams_of[5], part), 71), part)
    small_order = draw_small_order(jax.random.fold_in(jax.random.fold_in(streams_of[5], part), 71), part)
    return dict(big_emb=big_emb, big_order=big_order, small_emb=small_emb, small_clus=small_clus, small_order=small_order)


def normalize(values):
    floats = values.astype(jnp.float32)
    squares = lax.optimization_barrier(jnp.sum(floats * floats, axis=-1, keepdims=True))
    return (floats * lax.rsqrt(squares + 1e-06)).astype(jnp.bfloat16)

def best_over(row_emb, row_ord, col_emb, col_ord):
    total_rows = row_emb.shape[0]
    height = 512 if total_rows % 512 == 0 else total_rows

    def one_block(block_at):
        rows_here = lax.dynamic_slice_in_dim(row_emb, block_at * height, height, 0)
        ord_here = lax.dynamic_slice_in_dim(row_ord, block_at * height, height, 0)
        scores = lax.dot_general(rows_here, col_emb, (((1,), (1,)), ((), ())), preferred_element_type=jnp.float32)
        allowed = col_ord[None, :] < ord_here[:, None]
        return lax.optimization_barrier(jnp.max(jnp.where(allowed, scores, jnp.float32(-1.0)), axis=1))
    blocks = lax.map(one_block, jnp.arange(total_rows // height, dtype=jnp.int32))
    return jnp.maximum(blocks.reshape(total_rows), jnp.float32(-1.0))

def cluster_best(slots, clusters, orders):
    scores = lax.dot_general(slots, slots, (((1,), (1,)), ((), ())), preferred_element_type=jnp.float32)
    allowed = (clusters[None, :] == clusters[:, None]) & (clusters[:, None] >= 0) & (orders[None, :] < orders[:, None])
    return lax.optimization_barrier(jnp.max(jnp.where(allowed, scores, jnp.float32(-1.0)), axis=1))

def reference(big_emb, big_order, small_emb, small_clus, small_order):
    big_unit = normalize(big_emb)
    big_best = best_over(big_unit, big_order, big_unit, big_order)
    small_unit = normalize(small_emb)
    emb_five = small_unit.reshape(N_ROWS, N_COLS, N_ROWS, CAP, D).transpose(2, 1, 0, 3, 4)
    emb_dest = emb_five.reshape(N_ROWS * N_COLS, N_ROWS * CAP, D)
    clus_dest = small_clus.reshape(N_ROWS, N_COLS, N_ROWS, CAP).transpose(2, 1, 0, 3).reshape(N_ROWS * N_COLS, N_ROWS * CAP)
    ord_dest = small_order.reshape(N_ROWS, N_COLS, N_ROWS, CAP).transpose(2, 1, 0, 3).reshape(N_ROWS * N_COLS, N_ROWS * CAP)

    def per_dest(inputs):
        return cluster_best(inputs[0], inputs[1], inputs[2])
    results = lax.map(per_dest, (emb_dest, clus_dest, ord_dest))
    small_best = results.reshape(N_ROWS, N_COLS, N_ROWS, CAP).transpose(2, 1, 0, 3).reshape(N_ROWS * N_COLS, N_ROWS, CAP)
    return (big_best, small_best)
```

```python
import functools

import jax
import jax.numpy as jnp
from jax import lax
from jax.experimental import pallas as pl
from jax.experimental.pallas import tpu as pltpu
from jax.sharding import PartitionSpec as P

F32, BF16 = jnp.float32, jnp.bfloat16
BOTH = ("rows", "cols")
NT = (((1,), (1,)), ((), ()))
NN = (((1,), (0,)), ((), ()))
META = 8
DIGIT = 256


def normalize(values):
    floats = values.astype(F32)
    squares = jnp.sum(floats * floats, axis=-1, keepdims=True)
    return (floats * lax.rsqrt(squares + 1e-06)).astype(BF16)


def best_over(row_emb, row_ord, col_emb, col_ord):
    total_rows = row_emb.shape[0]
    height = 512 if total_rows % 512 == 0 else total_rows

    def one_block(block_at):
        rows_here = lax.dynamic_slice_in_dim(row_emb, block_at * height, height, 0)
        ord_here = lax.dynamic_slice_in_dim(row_ord, block_at * height, height, 0)
        scores = lax.dot_general(rows_here, col_emb, NT, preferred_element_type=F32)
        allowed = col_ord[None, :] < ord_here[:, None]
        return jnp.max(jnp.where(allowed, scores, F32(-1.0)), axis=1)

    blocks = lax.map(one_block, jnp.arange(total_rows // height, dtype=jnp.int32))
    return jnp.maximum(blocks.reshape(total_rows), F32(-1.0))


def cluster_best(slots, clusters, orders):
    scores = lax.dot_general(slots, slots, NT, preferred_element_type=F32)
    allowed = (
        (clusters[None, :] == clusters[:, None])
        & (clusters[:, None] >= 0)
        & (orders[None, :] < orders[:, None])
    )
    return jnp.max(jnp.where(allowed, scores, F32(-1.0)), axis=1)


def local_any(big_emb, big_order, small_emb, small_clus, small_order):
    own_rows = big_emb.shape[0]
    big_unit = normalize(big_emb)
    small_unit = normalize(small_emb)
    sent_emb, sent_clus, sent_ord = (
        lax.all_to_all(v, "rows", split_axis=1, concat_axis=1, tiled=True)
        for v in (small_unit, small_clus, small_order)
    )
    depth = sent_emb.shape[1] * sent_emb.shape[2]
    slot_best = cluster_best(
        sent_emb.reshape(depth, sent_emb.shape[3]),
        sent_clus.reshape(depth),
        sent_ord.reshape(depth),
    )
    slot_best = slot_best.reshape(sent_clus.shape)
    partial_value = best_over(
        lax.all_gather(big_unit, "cols", axis=0, tiled=True),
        lax.all_gather(big_order, "cols", axis=0, tiled=True),
        lax.all_gather(big_unit, "rows", axis=0, tiled=True),
        lax.all_gather(big_order, "rows", axis=0, tiled=True),
    )
    merged = lax.pmax(partial_value, "cols")
    big_best = lax.dynamic_slice_in_dim(merged, lax.axis_index("cols") * own_rows, own_rows, 0)
    small_best = lax.all_to_all(slot_best, "rows", split_axis=1, concat_axis=1, tiled=True)
    return (big_best, small_best)


def call(kernel, name, outs, *args, flops=0):
    moved = sum(a.size * a.dtype.itemsize for a in args)
    return pl.pallas_call(
        kernel,
        name=name,
        out_shape=outs,
        in_specs=[pl.BlockSpec(memory_space=pltpu.VMEM)] * len(args),
        out_specs=jax.tree.map(lambda _: pl.BlockSpec(memory_space=pltpu.VMEM), outs),
        compiler_params=pltpu.CompilerParams(vmem_limit_bytes=24 << 20),
        cost_estimate=pl.CostEstimate(flops=flops, bytes_accessed=moved, transcendentals=0),
    )(*args)


def unit(values):
    floats = values.astype(F32)
    squares = jnp.sum(floats * floats, axis=-1, keepdims=True)
    return (floats * lax.rsqrt(squares + 1e-06)).astype(BF16)


def prep_big(x_ref, o_ref, out_ref):
    n, d = x_ref.shape
    out_ref[0:n, :] = unit(x_ref[...])
    order = o_ref[...]
    hi = jnp.broadcast_to((order >> 8).astype(F32), (META, n))
    lo = jnp.broadcast_to((order & (DIGIT - 1)).astype(F32), (META, n))
    row = lax.broadcasted_iota(jnp.int32, (META, n), 0)
    out_ref[n:, 0:n] = jnp.where(row == 0, hi, jnp.where(row == 1, lo, 0.0)).astype(BF16)
    if d > n:
        out_ref[n:, n:] = jnp.zeros((META, d - n), BF16)


def order_row(ref):
    n = ref.shape[0] - META
    digits = ref[n:, 0:n].astype(F32)
    return digits[0:1] * DIGIT + digits[1:2]


def order_col(ref):
    row = order_row(ref)
    n = row.shape[1]
    return jnp.broadcast_to(row, (128, n)).T[:, 0:1]


def scores_of(y_ref, x_ref):
    n = x_ref.shape[0] - META
    return lax.dot_general(y_ref[0:n, :], x_ref[0:n, :], NT, preferred_element_type=F32)


def inner_kernel(*refs):
    *blocks, out_ref = refs
    own = order_row(blocks[0])
    best = None
    for y in blocks:
        s = jnp.where(order_col(y) < own, scores_of(y, blocks[0]), F32(-1.0))
        best = s if best is None else jnp.maximum(best, s)
    out_ref[...] = jnp.max(best, axis=0, keepdims=True)


def sweep(x_ref, y_refs, cols):
    own = order_col(x_ref)
    best = None
    for at, y in y_refs:
        s = scores_of(x_ref, y)
        later = order_row(y) < own
        mine = jnp.where(later, s, F32(-1.0))
        best = mine if best is None else jnp.maximum(best, mine)
        other = jnp.max(jnp.where(later, F32(-1.0), s), axis=0, keepdims=True)
        cols[at : at + 1, :] = jnp.maximum(cols[at : at + 1, :], other)
    n = best.shape[1]
    folded = functools.reduce(jnp.maximum, [best[:, j : j + 128] for j in range(0, n, 128)])
    return jnp.max(folded.T, axis=0, keepdims=True)


PLANE = (0, 1, 2, 3)
RIGHT = (4, 5, 6, 7)
ROW_T, ROW_A, ROW_B = 8, 9, 10
TABLE = 16


def place():
    r = lax.axis_index("rows")
    return r // 2, r % 2, lax.axis_index("cols")


def early_kernel(own, c, x, xc, t, tc, a, cols_ref):
    z, _, _ = place()
    cols_ref[...] = jnp.full(cols_ref.shape, -1.0, F32)
    plane = list(zip(PLANE, (own, c, x, xc)))

    @pl.when(z % 2 == 0)
    def _():
        cols_ref[ROW_T : ROW_T + 1, :] = sweep(t, plane, cols_ref)

    @pl.when(z == 2)
    def _():
        cols_ref[ROW_A : ROW_A + 1, :] = sweep(a, plane + list(zip(RIGHT, (t, tc))), cols_ref)


def late_kernel(own, c, x, xc, t, tc, d, dc, a, b, cols_ref, small_ref, p1, p2, p3, p4, p5, p6, p7, p8, p9, mine, work):
    z, _, _ = place()
    work[...] = cols_ref[...]

    @pl.when(z == 2)
    def _():
        far = list(zip(RIGHT, (t, tc, d, dc)))
        plane = list(zip(PLANE, (own, c, x, xc)))
        more = sweep(a, far[2:], work)
        work[ROW_A : ROW_A + 1, :] = jnp.maximum(work[ROW_A : ROW_A + 1, :], more)
        work[ROW_B : ROW_B + 1, :] = sweep(b, plane + far, work)

    for ref, at in ((mine, 0), (p1, 1), (p2, 2), (p3, 3), (p5, 5), (p6, 6), (p7, 7)):
        ref[...] = work[at : at + 1, :]
    near = jnp.maximum(work[4:5, :], work[ROW_T : ROW_T + 1, :])
    for ref, row in ((p4, near), (p8, work[ROW_A : ROW_A + 1, :]), (p9, work[ROW_B : ROW_B + 1, :])):
        ref[0:8, :] = jnp.broadcast_to(row, (8, row.shape[1]))
        ref[8:16, 0:128] = small_ref[...]


def prep_small(mine, other, clus, oclus, order, oorder, out_ref):
    dests, cap, d = mine.shape
    z, k, _ = place()
    chips = dests // 2
    half = chips * cap
    for src, base in ((mine, k), (other, 1 - k)):
        for j in range(chips):
            at = pl.multiple_of(base * half + j * cap, cap)
            out_ref[pl.ds(at, cap), :] = unit(src[2 * j + k])
    lanes = dests * cap
    pick_r = lax.broadcasted_iota(jnp.int32, (META, dests), 0)
    pick_c = lax.broadcasted_iota(jnp.int32, (META, dests), 1)
    pick = jnp.where(pick_c == 2 * pick_r + k, 1.0, 0.0).astype(BF16)
    slot = lax.broadcasted_iota(jnp.int32, (cap, lanes), 0)
    lane = lax.broadcasted_iota(jnp.int32, (cap, lanes), 1)

    def placed(values, base):
        rows = lax.dot_general(pick, values.astype(F32).astype(BF16), NN, preferred_element_type=F32)
        spread = jnp.where(lane == slot + (2 * z + base) * cap, 1.0, 0.0).astype(BF16)
        return lax.dot_general(rows.astype(BF16), spread, NN, preferred_element_type=F32)

    for at, pair in enumerate(
        (
            (clus[...], oclus[...]),
            (order[...] >> 8, oorder[...] >> 8),
            (order[...] & (DIGIT - 1), oorder[...] & (DIGIT - 1)),
        )
    ):
        both = placed(pair[0], k) + placed(pair[1], 1 - k)
        out_ref[2 * half :, at * lanes : (at + 1) * lanes] = both.astype(BF16)
    out_ref[2 * half :, 3 * lanes :] = jnp.zeros((META, d - 3 * lanes), BF16)


def small_kernel(p0, p1, p2, p3, out_ref):
    z, _, _ = place()
    rows = p0.shape[0] - META
    chips, half = 4, rows // 2
    cap = half // chips
    lanes = 2 * chips * cap
    out_ref[...] = jnp.full(out_ref.shape, -1.0, F32)

    @pl.when(z == 1)
    def _():
        parts = (p0, p1, p2, p3)
        meta = sum(p[rows:, 0 : 3 * lanes].astype(F32) for p in parts)
        clus = meta[:, 0:lanes]
        order = meta[:, lanes : 2 * lanes] * DIGIT + meta[:, 2 * lanes :]
        clus_t, order_t = clus.T, order.T
        for j in range(chips):
            slots = jnp.concatenate(
                [p[k * half + j * cap : k * half + (j + 1) * cap, :] for p in parts for k in range(2)], axis=0
            )
            s = lax.dot_general(slots, slots, NT, preferred_element_type=F32)
            allowed = (
                (clus_t[:, j : j + 1] == clus[j : j + 1, :])
                & (clus[j : j + 1, :] >= 0)
                & (order_t[:, j : j + 1] < order[j : j + 1, :])
            )
            out_ref[j : j + 1, :] = jnp.max(jnp.where(allowed, s, F32(-1.0)), axis=0, keepdims=True)


def join_kernel(own, other, out_ref):
    _, k, _ = place()
    chips = 4
    a, b = own[0:chips, :], other[0:chips, :]
    first = k == 0
    out_ref[0:chips, :] = jnp.where(first, a, b)
    out_ref[chips:, :] = jnp.where(first, b, a)


def final_kernel(inner, mine, small, g1, g2, g3, g4, g5, g6, g7, g8, g9, big_ref, small_ref):
    z, k, _ = place()
    best = functools.reduce(jnp.maximum, [v[...] for v in (inner, mine, g1, g2, g3)])

    def take(when, row):
        return jnp.where(when, row, F32(-1.0))

    best = jnp.maximum(best, take(z != 2, g4[0:1, :]))
    for g in (g5, g6, g7):
        best = jnp.maximum(best, take(z == 3, g[...]))
    best = jnp.maximum(best, take((z == 1) | (z == 2), g8[0:1, :]))
    best = jnp.maximum(best, take((z == 0) | (z == 3), g9[0:1, :]))
    big_ref[...] = best

    dests, cap = small_ref.shape
    lanes = small.shape[1]
    got = jnp.where(
        z == 1,
        small[...],
        jnp.where(z == 2, g8[8:16, 0:lanes], jnp.where(z == 3, g9[8:16, 0:lanes], g4[8:16, 0:lanes])),
    )
    turned = pltpu.roll(got, lanes - (2 * z + k) * cap, 1)[:, 0:cap]
    chips = dests // 2
    for j in range(chips):
        for q in range(2):
            small_ref[2 * j + q : 2 * j + q + 1, :] = turned[q * chips + j : q * chips + j + 1, :]


def local_line(big_emb, big_order, small_emb, small_clus, small_order):
    n, d = big_emb.shape
    _, dests, cap, _ = small_emb.shape
    chips = dests // 2
    lanes = dests * cap

    def move(value, to):
        pairs = []
        for z in range(chips):
            for k in range(2):
                for x in range(2):
                    t = to(z, k, x)
                    if t is not None:
                        pairs.append(((2 * z + k) * 2 + x, (2 * t[0] + t[1]) * 2 + t[2]))
        return lax.ppermute(value, BOTH, pairs)

    def hop(value, targets):
        return move(value, lambda z, k, x: (targets[z], k, x) if z in targets else None)

    def core(value):
        return move(value, lambda z, k, x: (z, 1 - k, x))

    def col(value):
        return move(value, lambda z, k, x: (z, k, 1 - x))

    block = jax.ShapeDtypeStruct((n + META, d), BF16)
    row = jax.ShapeDtypeStruct((1, n), F32)

    s_emb = small_emb.reshape(dests, cap, d)
    s_clus, s_ord = small_clus.reshape(dests, cap), small_order.reshape(dests, cap)
    o_emb, o_clus, o_ord = core(s_emb), core(s_clus), core(s_ord)

    own = call(prep_big, "prep_big", block, big_emb, big_order.reshape(1, n))
    b = hop(own, {0: 2})
    a = hop(own, {1: 2})
    t = hop(own, {3: 2, 1: 0})
    x = col(own)
    dg = move(own, lambda z, k, x: (2, k, 1 - x) if z == 3 else None)
    c = core(own)

    half = chips * cap
    sp = call(
        prep_small,
        "prep_small",
        jax.ShapeDtypeStruct((2 * half + META, d), BF16),
        s_emb, o_emb, s_clus, o_clus, s_ord, o_ord,
    )
    s0, s2, s3 = hop(sp, {0: 1}), hop(sp, {2: 1}), hop(sp, {3: 1})

    xc, tc, dc = core(x), core(t), core(dg)
    pair = 2 * n * n * d
    inner = call(inner_kernel, "inner", row, own, c, x, xc, flops=4 * pair)
    table = jax.ShapeDtypeStruct((TABLE, n), F32)
    cols = call(early_kernel, "early", table, own, c, x, xc, t, tc, a, flops=10 * pair)

    best = call(
        small_kernel, "small", jax.ShapeDtypeStruct((8, lanes), F32), s0, sp, s2, s3, flops=chips * 2 * lanes * lanes * d
    )
    other = move(best, lambda z, k, x: (z, 1 - k, x) if z == 1 else None)
    small = call(join_kernel, "join", jax.ShapeDtypeStruct((8, lanes), F32), best, other)

    big_pay = jax.ShapeDtypeStruct((16, n), F32)
    outs = (row, row, row, big_pay, row, row, row, big_pay, big_pay, row)
    args = (own, c, x, xc, t, tc, dg, dc, a, b, cols, small)
    *p, mine = pl.pallas_call(
        late_kernel,
        name="late",
        out_shape=outs,
        in_specs=[pl.BlockSpec(memory_space=pltpu.VMEM)] * len(args),
        out_specs=tuple(pl.BlockSpec(memory_space=pltpu.VMEM) for _ in outs),
        scratch_shapes=[pltpu.VMEM((TABLE, n), F32)],
        compiler_params=pltpu.CompilerParams(vmem_limit_bytes=24 << 20),
        cost_estimate=pl.CostEstimate(flops=10 * pair, bytes_accessed=10 * n * d * 2, transcendentals=0),
    )(*args)
    p1, p2, p3, p4, p5, p6, p7, p8, p9 = p
    g9 = hop(p9, {2: 0, 1: 3})
    g8 = hop(p8, {2: 1, 1: 2})
    g4 = hop(p4, {2: 3, 0: 1, 1: 0})
    g7 = move(p7, lambda z, k, x: (3, 1 - k, 1 - x) if z == 2 else None)
    g6 = move(p6, lambda z, k, x: (3, k, 1 - x) if z == 2 else None)
    g5 = move(p5, lambda z, k, x: (3, 1 - k, x) if z == 2 else None)
    g3 = move(p3, lambda z, k, x: (z, 1 - k, 1 - x))
    g2, g1 = col(p2), core(p1)
    big, sm = call(
        final_kernel, "final", (row, jax.ShapeDtypeStruct((dests, cap), F32)),
        inner, mine, small, g1, g2, g3, g4, g5, g6, g7, g8, g9,
    )
    return big.reshape(n), sm.reshape(1, dests, cap)


def solution(mesh):
    placed = (
        P(("groups", "rows", "cols"), None),
        P(("groups", "rows", "cols")),
        P(("groups", "rows", "cols"), None, None, None),
        P(("groups", "rows", "cols"), None, None),
        P(("groups", "rows", "cols"), None, None),
    )
    line = mesh.shape["rows"] == 8 and mesh.shape["cols"] == 2
    return jax.shard_map(
        local_line if line else local_any,
        mesh=mesh,
        in_specs=placed,
        out_specs=(P(("groups", "rows", "cols")), P(("groups", "rows", "cols"), None, None)),
        check_vma=False,
    )
```

```python
import functools

import jax
import jax.numpy as jnp
from jax import lax
from jax.experimental import pallas as pl
from jax.experimental.pallas import tpu as pltpu
from jax.sharding import PartitionSpec as P


F32, BF16 = jnp.float32, jnp.bfloat16
BOTH = ("rows", "cols")
NT = (((1,), (1,)), ((), ()))
NN = (((1,), (0,)), ((), ()))
META = 8
DIGIT = 256


def normalize(values):
    floats = values.astype(F32)
    squares = jnp.sum(floats * floats, axis=-1, keepdims=True)
    return (floats * lax.rsqrt(squares + 1e-06)).astype(BF16)


def best_over(row_emb, row_ord, col_emb, col_ord):
    total_rows = row_emb.shape[0]
    height = 512 if total_rows % 512 == 0 else total_rows

    def one_block(block_at):
        rows_here = lax.dynamic_slice_in_dim(row_emb, block_at * height, height, 0)
        ord_here = lax.dynamic_slice_in_dim(row_ord, block_at * height, height, 0)
        scores = lax.dot_general(rows_here, col_emb, NT, preferred_element_type=F32)
        allowed = col_ord[None, :] < ord_here[:, None]
        return jnp.max(jnp.where(allowed, scores, F32(-1.0)), axis=1)

    blocks = lax.map(one_block, jnp.arange(total_rows // height, dtype=jnp.int32))
    return jnp.maximum(blocks.reshape(total_rows), F32(-1.0))


def cluster_best(slots, clusters, orders):
    scores = lax.dot_general(slots, slots, NT, preferred_element_type=F32)
    allowed = (
        (clusters[None, :] == clusters[:, None])
        & (clusters[:, None] >= 0)
        & (orders[None, :] < orders[:, None])
    )
    return jnp.max(jnp.where(allowed, scores, F32(-1.0)), axis=1)


def local_any(big_emb, big_order, small_emb, small_clus, small_order):
    own_rows = big_emb.shape[0]
    big_unit = normalize(big_emb)
    small_unit = normalize(small_emb)
    sent_emb, sent_clus, sent_ord = (
        lax.all_to_all(v, "rows", split_axis=1, concat_axis=1, tiled=True)
        for v in (small_unit, small_clus, small_order)
    )
    depth = sent_emb.shape[1] * sent_emb.shape[2]
    slot_best = cluster_best(
        sent_emb.reshape(depth, sent_emb.shape[3]),
        sent_clus.reshape(depth),
        sent_ord.reshape(depth),
    )
    slot_best = slot_best.reshape(sent_clus.shape)
    partial_value = best_over(
        lax.all_gather(big_unit, "cols", axis=0, tiled=True),
        lax.all_gather(big_order, "cols", axis=0, tiled=True),
        lax.all_gather(big_unit, "rows", axis=0, tiled=True),
        lax.all_gather(big_order, "rows", axis=0, tiled=True),
    )
    merged = lax.pmax(partial_value, "cols")
    big_best = lax.dynamic_slice_in_dim(merged, lax.axis_index("cols") * own_rows, own_rows, 0)
    small_best = lax.all_to_all(slot_best, "rows", split_axis=1, concat_axis=1, tiled=True)
    return (big_best, small_best)


def call(kernel, outs, *args, flops=0, scratch=(), space=pltpu.VMEM):
    moved = sum(a.size * a.dtype.itemsize for a in args)
    return pl.pallas_call(
        kernel,
        out_shape=outs,
        in_specs=[pl.BlockSpec(memory_space=space)] * len(args),
        out_specs=jax.tree.map(lambda _: pl.BlockSpec(memory_space=pltpu.VMEM), outs),
        scratch_shapes=list(scratch),
        compiler_params=pltpu.CompilerParams(vmem_limit_bytes=24 << 20),
        cost_estimate=pl.CostEstimate(flops=flops, bytes_accessed=moved, transcendentals=0),
    )(*args)


def place():
    r = lax.axis_index("rows")
    return r // 2, r % 2, lax.axis_index("cols")


def unit(values):
    floats = values.astype(F32)
    squares = jnp.sum(floats * floats, axis=-1, keepdims=True)
    return (floats * lax.rsqrt(squares + 1e-06)).astype(BF16)


def prep_small_kernel(s_ref, clus_ref, ord_ref, out):
    dests, cap, d = s_ref.shape
    z, k, _ = place()
    lanes = dests * cap
    slot = lax.broadcasted_iota(jnp.int32, (cap, lanes), 0)
    lane = lax.broadcasted_iota(jnp.int32, (cap, lanes), 1)
    spread = jnp.where(lane == slot + k * (lanes // 2) + z * cap, 1.0, 0.0).astype(BF16)
    for j in range(dests):
        out[j * cap : (j + 1) * cap, :] = unit(s_ref[j])
    orders = ord_ref[...]
    for at, digits in enumerate((clus_ref[...], orders >> 8, orders & (DIGIT - 1))):
        rows = lax.dot_general(digits.astype(F32).astype(BF16), spread, NN, preferred_element_type=F32)
        out[lanes:, at * lanes : (at + 1) * lanes] = rows.astype(BF16)
    out[lanes:, 3 * lanes :] = jnp.zeros((META, d - 3 * lanes), BF16)


def prep_kernel(x_ref, meta_ref, own):
    n, _ = x_ref.shape
    own[0:n, :] = unit(x_ref[...])
    own[n:, :] = meta_ref[...]


def order_row(ref):
    n = ref.shape[0] - META
    digits = ref[n:, 0:n].astype(F32)
    return digits[0:1] * DIGIT + digits[1:2]


def order_col(ref):
    row = order_row(ref)
    n = row.shape[1]
    return jnp.broadcast_to(row, (128, n)).T[:, 0:1]


def scores_of(y_ref, x_ref):
    n = x_ref.shape[0] - META
    return lax.dot_general(y_ref[0:n, :], x_ref[0:n, :], NT, preferred_element_type=F32)


def sweep(x_ref, y_refs, cols):
    own = order_col(x_ref)
    best = None
    for at, y in y_refs:
        s = scores_of(x_ref, y)
        later = order_row(y) < own
        mine = jnp.where(later, s, F32(-1.0))
        best = mine if best is None else jnp.maximum(best, mine)
        other = jnp.max(jnp.where(later, F32(-1.0), s), axis=0, keepdims=True)
        cols[at : at + 1, :] = jnp.maximum(cols[at : at + 1, :], other)
    n = best.shape[1]
    folded = functools.reduce(jnp.maximum, [best[:, j : j + 128] for j in range(0, n, 128)])
    return jnp.max(folded.T, axis=0, keepdims=True)


PLANE = (0, 4, 1, 5)
RIGHT = (2, 6, 3, 7)
ROW_T, ROW_A, ROW_B = 8, 9, 10
TABLE = 16


def plane_kernel(own, c, x, xc, t, cols_ref, inner_ref):
    z, _, _ = place()
    cols_ref[...] = jnp.full(cols_ref.shape, -1.0, F32)
    mine = order_row(own)
    best = None
    for y in (own, c, x, xc):
        s = jnp.where(order_col(y) < mine, scores_of(y, own), F32(-1.0))
        best = s if best is None else jnp.maximum(best, s)
    inner_ref[...] = jnp.max(best, axis=0, keepdims=True)

    @pl.when(z % 2 == 0)
    def _():
        cols_ref[ROW_T : ROW_T + 1, :] = sweep(t, list(zip(PLANE, (own, c, x, xc))), cols_ref)


def left_kernel(result, own, c, x, xc, t, tc, block, cols_ref, out_ref):
    z, _, _ = place()
    out_ref[...] = cols_ref[...]

    @pl.when(z == 2)
    def _():
        met = list(zip(PLANE, (own, c, x, xc))) + list(zip(RIGHT, (t, tc)))
        out_ref[result : result + 1, :] = sweep(block, met, out_ref)


def late_kernel(d, dc, a, b, cols_ref, small_ref, keep, swap, p2, p3):
    z, _, _ = place()
    keep[...] = cols_ref[...]

    @pl.when(z == 2)
    def _():
        far = list(zip(RIGHT[2:], (d, dc)))
        for block, at in ((a, ROW_A), (b, ROW_B)):
            row = sweep(block, far, keep)
            keep[at : at + 1, :] = jnp.maximum(keep[at : at + 1, :], row)

    swap[...] = keep[4:8, :]
    for ref, at in ((p2, ROW_A), (p3, ROW_B)):
        ref[0:8, :] = jnp.broadcast_to(keep[at : at + 1, :], (8, keep.shape[1]))
        ref[8:16, 0:128] = small_ref[...]


def merge_kernel(keep, other, small_ref, mine, px, p1, p1x):
    got = jnp.maximum(keep[0:4, :], other[...])
    mine[...] = got[0:1]
    px[...] = got[1:2]
    p1x[...] = got[3:4]
    row = jnp.maximum(got[2:3], keep[ROW_T : ROW_T + 1, :])
    p1[0:8, :] = jnp.broadcast_to(row, (8, row.shape[1]))
    p1[8:16, 0:128] = small_ref[...]


def small_kernel(own, own_c, p0, c0, p2, c2, p3, c3, out_ref):
    z, k, _ = place()
    lanes = own.shape[0] - META
    dests, cap = META, lanes // META
    out_ref[...] = jnp.full(out_ref.shape, -1.0, F32)

    @pl.when(z == 1)
    def _():
        mine, others = (p0, own, p2, p3), (c0, own_c, c2, c3)
        meta = sum(p[lanes:, 0 : 3 * lanes].astype(F32) for p in mine + others)
        clus = meta[:, 0:lanes]
        order = meta[:, lanes : 2 * lanes] * DIGIT + meta[:, 2 * lanes :]
        clus_t, order_t = clus.T, order.T
        first = k == 0
        for j in range(dests):
            at = slice(j * cap, (j + 1) * cap)
            a = jnp.concatenate([p[at, :] for p in mine], axis=0)
            b = jnp.concatenate([p[at, :] for p in others], axis=0)
            slots = jnp.concatenate([jnp.where(first, a, b), jnp.where(first, b, a)], axis=0)
            s = lax.dot_general(slots, slots, NT, preferred_element_type=F32)
            allowed = (
                (clus_t[:, j : j + 1] == clus[j : j + 1, :])
                & (clus[j : j + 1, :] >= 0)
                & (order_t[:, j : j + 1] < order[j : j + 1, :])
            )
            out_ref[j : j + 1, :] = jnp.max(jnp.where(allowed, s, F32(-1.0)), axis=0, keepdims=True)


def final_kernel(inner, mine, small, gx, g1, g1x, g2, g3, big_ref, small_ref):
    z, k, _ = place()
    none = F32(-1.0)
    rows = [v[...] for v in (inner, mine, gx)] + [v[0:1, :] for v in (g1, g2)]
    best = functools.reduce(jnp.maximum, rows)
    best = jnp.maximum(best, jnp.where(z == 3, g1x[...], none))
    big_ref[...] = jnp.maximum(best, jnp.where(z == 0, g3[0:1, :], none))

    _, cap = small_ref.shape
    lanes = small.shape[1]
    near = jnp.where(z == 0, g1[8:16, 0:lanes], small[...])
    got = jnp.where(z == 2, g2[8:16, 0:lanes], jnp.where(z == 3, g3[8:16, 0:lanes], near))
    small_ref[...] = pltpu.roll(got, lanes - (k * (lanes // 2) + z * cap), 1)[:, 0:cap]


def line_body(big_emb, big_order, small_emb, small_clus, small_order):
    n, d = big_emb.shape
    _, dests, cap, _ = small_emb.shape
    chips = dests // 2
    lanes = dests * cap

    def move(value, to):
        pairs = []
        for z in range(chips):
            for k in range(2):
                for x in range(2):
                    t = to(z, k, x)
                    if t is not None:
                        pairs.append(((2 * z + k) * 2 + x, (2 * t[0] + t[1]) * 2 + t[2]))
        return lax.ppermute(value, BOTH, pairs)

    def hop(value, targets):
        return move(value, lambda z, k, x: (targets[z], k, x) if z in targets else None)

    def core(value):
        return move(value, lambda z, k, x: (z, 1 - k, x))

    def col(value):
        return move(value, lambda z, k, x: (z, k, 1 - x))

    def shape(rows, cols, kind=F32):
        return jax.ShapeDtypeStruct((rows, cols), kind)

    pair = 2 * n * n * d
    s_emb = small_emb.reshape(dests, cap, d)
    s_clus, s_ord = small_clus.reshape(dests, cap), small_order.reshape(dests, cap)
    block, part = shape(n + META, d, BF16), shape(n // 2 + META, d, BF16)
    digits = jnp.stack([big_order >> 8, big_order & (DIGIT - 1)]).astype(F32).astype(BF16)
    meta = jnp.pad(digits, ((0, META - 2), (0, d - n)))
    own = call(prep_kernel, block, big_emb, meta)
    a = hop(own, {1: 2})
    t = hop(own, {3: 2, 1: 0})
    x = col(own)
    b = hop(own, {0: 2})
    c = core(own)

    s1 = call(prep_small_kernel, part, s_emb, s_clus, s_ord)
    s0, s3, s2 = hop(s1, {0: 1}), hop(s1, {3: 1}), hop(s1, {2: 1})
    s1c = core(s1)
    xc, tc = core(x), core(t)
    forward = jnp.where(lax.axis_index("rows") // 2 == 3, x, t)
    relay = {(3, 0): lambda x: (2, 0, x), (2, 1): lambda x: (2, 1, 1 - x)}
    dg = move(forward, lambda z, k, x: relay[z, k](x) if (z, k) in relay else None)
    dc = core(dg)

    plane = (own, c, x, xc, t)
    table = shape(TABLE, n)
    cols, inner = call(plane_kernel, (table, shape(1, n)), *plane, flops=8 * pair)
    s0c, s2c, s3c = core(s0), core(s2), core(s3)
    small = call(
        small_kernel,
        shape(8, lanes),
        s1, s1c, s0, s0c, s2, s2c, s3, s3c,
        flops=dests * 2 * lanes * lanes * d,
    )

    for row, left in ((ROW_A, a), (ROW_B, b)):
        cols = call(functools.partial(left_kernel, row), table, *plane, tc, left, cols, flops=6 * pair)
    keep, swap, r2, r3 = call(
        late_kernel,
        (table, shape(4, n), shape(16, n), shape(16, n)),
        dg, dc, a, b, cols, small,
        flops=4 * pair,
    )
    got = core(swap)
    g3 = hop(r3, {2: 0, 1: 3})
    mine, rx, r1, r1x = call(
        merge_kernel, (shape(1, n), shape(1, n), shape(16, n), shape(1, n)), keep, got, small
    )
    g1x = move(r1x, lambda z, k, x: (3, k, 1 - x) if z == 2 else None)
    g1 = hop(r1, {2: 3, 3: 2, 0: 1, 1: 0})
    g2 = hop(r2, {1: 2, 2: 1, 0: 0, 3: 3})
    gx = col(rx)
    big, sm = call(
        final_kernel, (shape(1, n), shape(dests, cap)), inner, mine, small, gx, g1, g1x, g2, g3
    )
    return big.reshape(n), sm.reshape(1, dests, cap)


def fits(mesh, n, dests, cap):
    rows, cols = mesh.shape["rows"], mesh.shape["cols"]
    return rows == 8 and cols == 2 and dests == META and n == 2 * dests * cap and n == DIGIT


def solution(mesh):
    placed = (
        P(("groups", "rows", "cols"), None),
        P(("groups", "rows", "cols")),
        P(("groups", "rows", "cols"), None, None, None),
        P(("groups", "rows", "cols"), None, None),
        P(("groups", "rows", "cols"), None, None),
    )
    parts = mesh.size

    def over(local):
        return jax.shard_map(
            local,
            mesh=mesh,
            in_specs=placed,
            out_specs=(P(("groups", "rows", "cols")), P(("groups", "rows", "cols"), None, None)),
            check_vma=False,
        )

    line = over(line_body)

    def step(big_emb, big_order, small_emb, small_clus, small_order):
        args = (big_emb, big_order, small_emb, small_clus, small_order)
        ok = fits(mesh, big_emb.shape[0] // parts, small_emb.shape[1], small_emb.shape[2])
        return line(*args) if ok else over(local_any)(*args)

    return step
```

```python
import functools

import jax
import jax.numpy as jnp
from jax import lax
from jax.experimental import pallas as pl
from jax.experimental.pallas import tpu as pltpu
from jax.sharding import PartitionSpec as P


F32, BF16 = jnp.float32, jnp.bfloat16
BOTH = ("rows", "cols")
NT = (((1,), (1,)), ((), ()))
NN = (((1,), (0,)), ((), ()))
META = 8
DIGIT = 256


def normalize(values):
    floats = values.astype(F32)
    squares = jnp.sum(floats * floats, axis=-1, keepdims=True)
    return (floats * lax.rsqrt(squares + 1e-06)).astype(BF16)


def best_over(row_emb, row_ord, col_emb, col_ord):
    total_rows = row_emb.shape[0]
    height = 512 if total_rows % 512 == 0 else total_rows

    def one_block(block_at):
        rows_here = lax.dynamic_slice_in_dim(row_emb, block_at * height, height, 0)
        ord_here = lax.dynamic_slice_in_dim(row_ord, block_at * height, height, 0)
        scores = lax.dot_general(rows_here, col_emb, NT, preferred_element_type=F32)
        allowed = col_ord[None, :] < ord_here[:, None]
        return jnp.max(jnp.where(allowed, scores, F32(-1.0)), axis=1)

    blocks = lax.map(one_block, jnp.arange(total_rows // height, dtype=jnp.int32))
    return jnp.maximum(blocks.reshape(total_rows), F32(-1.0))


def cluster_best(slots, clusters, orders):
    scores = lax.dot_general(slots, slots, NT, preferred_element_type=F32)
    allowed = (
        (clusters[None, :] == clusters[:, None])
        & (clusters[:, None] >= 0)
        & (orders[None, :] < orders[:, None])
    )
    return jnp.max(jnp.where(allowed, scores, F32(-1.0)), axis=1)


def local_any(big_emb, big_order, small_emb, small_clus, small_order):
    own_rows = big_emb.shape[0]
    big_unit = normalize(big_emb)
    small_unit = normalize(small_emb)
    sent_emb, sent_clus, sent_ord = (
        lax.all_to_all(v, "rows", split_axis=1, concat_axis=1, tiled=True)
        for v in (small_unit, small_clus, small_order)
    )
    depth = sent_emb.shape[1] * sent_emb.shape[2]
    slot_best = cluster_best(
        sent_emb.reshape(depth, sent_emb.shape[3]),
        sent_clus.reshape(depth),
        sent_ord.reshape(depth),
    )
    slot_best = slot_best.reshape(sent_clus.shape)
    partial_value = best_over(
        lax.all_gather(big_unit, "cols", axis=0, tiled=True),
        lax.all_gather(big_order, "cols", axis=0, tiled=True),
        lax.all_gather(big_unit, "rows", axis=0, tiled=True),
        lax.all_gather(big_order, "rows", axis=0, tiled=True),
    )
    merged = lax.pmax(partial_value, "cols")
    big_best = lax.dynamic_slice_in_dim(merged, lax.axis_index("cols") * own_rows, own_rows, 0)
    small_best = lax.all_to_all(slot_best, "rows", split_axis=1, concat_axis=1, tiled=True)
    return (big_best, small_best)


def call(kernel, outs, *args, flops=0, scratch=(), space=pltpu.VMEM):
    moved = sum(a.size * a.dtype.itemsize for a in args)
    return pl.pallas_call(
        kernel,
        out_shape=outs,
        in_specs=[pl.BlockSpec(memory_space=space)] * len(args),
        out_specs=jax.tree.map(lambda _: pl.BlockSpec(memory_space=pltpu.VMEM), outs),
        scratch_shapes=list(scratch),
        compiler_params=pltpu.CompilerParams(vmem_limit_bytes=10 << 20),
        cost_estimate=pl.CostEstimate(flops=flops, bytes_accessed=moved, transcendentals=0),
    )(*args)


def place():
    r = lax.axis_index("rows")
    return r // 2, r % 2, lax.axis_index("cols")


def unit(values):
    floats = values.astype(F32)
    squares = jnp.sum(floats * floats, axis=-1, keepdims=True)
    return (floats * lax.rsqrt(squares + 1e-06)).astype(BF16)


def prep_small_kernel(s_ref, clus_ref, ord_ref, top, out, first):
    dests, cap, d = s_ref.shape
    z, k, _ = place()
    lanes = dests * cap
    slot = lax.broadcasted_iota(jnp.int32, (cap, lanes), 0)
    lane = lax.broadcasted_iota(jnp.int32, (cap, lanes), 1)
    spread = jnp.where(lane == slot + k * (lanes // 2) + z * cap, 1.0, 0.0).astype(BF16)
    for j in range(dests):
        out[j * cap : (j + 1) * cap, :] = unit(s_ref[j])
    orders = ord_ref[...]
    for at, digits in enumerate((clus_ref[...], orders >> 8, orders & (DIGIT - 1))):
        rows = lax.dot_general(digits.astype(F32).astype(BF16), spread, NN, preferred_element_type=F32)
        out[lanes:, at * lanes : (at + 1) * lanes] = rows.astype(BF16)
    out[lanes:, 3 * lanes :] = jnp.zeros((META, d - 3 * lanes), BF16)

    @pl.when(z == 2)
    def _():
        first[...] = out[...]

    @pl.when(z != 2)
    def _():
        first[...] = top[...]


def prep_kernel(x_ref, meta_ref, own, top, bot):
    n, _ = x_ref.shape
    own[0:n, :] = unit(x_ref[...])
    own[n:, :] = meta_ref[...]
    half = n // 2
    for ref, at in ((top, 0), (bot, half)):
        ref[0:half, :] = own[at : at + half, :]
        ref[half:, :] = meta_ref[...]


def order_row(ref):
    n = ref.shape[0] - META
    digits = ref[n:, 0:n].astype(F32)
    return digits[0:1] * DIGIT + digits[1:2]


def order_col(ref):
    row = order_row(ref)
    n = row.shape[1]
    return jnp.broadcast_to(row, (128, n)).T[:, 0:1]


def scores_of(y_ref, x_ref):
    n = x_ref.shape[0] - META
    return lax.dot_general(y_ref[0:n, :], x_ref[0:n, :], NT, preferred_element_type=F32)


def sweep(x_ref, y_refs, cols):
    own = order_col(x_ref)
    best = None
    for at, y in y_refs:
        s = scores_of(x_ref, y)
        later = order_row(y) < own
        mine = jnp.where(later, s, F32(-1.0))
        best = mine if best is None else jnp.maximum(best, mine)
        other = jnp.max(jnp.where(later, F32(-1.0), s), axis=0, keepdims=True)
        cols[at : at + 1, :] = jnp.maximum(cols[at : at + 1, :], other)
    n = best.shape[1]
    folded = functools.reduce(jnp.maximum, [best[:, j : j + 128] for j in range(0, n, 128)])
    return jnp.max(folded.T, axis=0, keepdims=True)


PLANE = (0, 4, 1, 5)
RIGHT = (2, 6, 3, 7)
ROW_T, ROW_A, ROW_B = 8, 9, 10
TABLE = 16


def plane_kernel(own, c, x, xc, t, cols_ref, inner_ref):
    z, _, _ = place()
    cols_ref[...] = jnp.full(cols_ref.shape, -1.0, F32)
    mine = order_row(own)
    best = None
    for y in (own, c, x, xc):
        s = jnp.where(order_col(y) < mine, scores_of(y, own), F32(-1.0))
        best = s if best is None else jnp.maximum(best, s)
    inner_ref[...] = jnp.max(best, axis=0, keepdims=True)

    @pl.when(z % 2 == 0)
    def _():
        cols_ref[ROW_T : ROW_T + 1, :] = sweep(t, list(zip(PLANE, (own, c, x, xc))), cols_ref)


def left(block, result, own, c, x, xc, t, tc, out_ref):
    met = list(zip(PLANE, (own, c, x, xc))) + list(zip(RIGHT, (t, tc)))
    out_ref[result : result + 1, :] = sweep(block, met, out_ref)


def left_a_kernel(own, c, x, xc, t, tc, a, cols_ref, out_ref):
    z, _, _ = place()
    out_ref[...] = cols_ref[...]

    @pl.when(z == 2)
    def _():
        left(a, ROW_A, own, c, x, xc, t, tc, out_ref)


def left_b_kernel(own, c, x, xc, t, tc, top, bot, cols_ref, out_ref, b):
    z, _, _ = place()
    out_ref[...] = cols_ref[...]

    @pl.when(z == 2)
    def _():
        n = b.shape[0] - META
        half = n // 2
        b[0:half, :] = top[0:half, :]
        b[half:n, :] = bot[0:half, :]
        b[n:, :] = top[half:, :]
        left(b, ROW_B, own, c, x, xc, t, tc, out_ref)


def pick_kernel(first, second, out):
    _, k, _ = place()
    for core, ref in enumerate((first, second)):

        @pl.when(k == core)
        def _(ref=ref):
            out[...] = ref[...]


def cross_kernel(cols, out):
    z, _, _ = place()
    for i, at in enumerate((1, 5, 2, 6)):
        out[i : i + 1, :] = cols[at : at + 1, :]

    @pl.when(z == 2)
    def _():
        out[2:3, :] = jnp.maximum(cols[2:3, :], cols[ROW_T : ROW_T + 1, :])


def late_kernel(d, dc, a, b, cols_ref, small_ref, keep, p2, p3):
    z, _, _ = place()
    keep[...] = cols_ref[...]

    @pl.when(z == 2)
    def _():
        far = list(zip(RIGHT[2:], (d, dc)))
        for block, at in ((a, ROW_A), (b, ROW_B)):
            row = sweep(block, far, keep)
            keep[at : at + 1, :] = jnp.maximum(keep[at : at + 1, :], row)

    first = jnp.where(z == 0, keep[ROW_T : ROW_T + 1, :], keep[ROW_B : ROW_B + 1, :])
    for ref, row in ((p2, keep[ROW_A : ROW_A + 1, :]), (p3, first)):
        ref[0:8, :] = jnp.broadcast_to(row, (8, row.shape[1]))
        ref[8:16, 0:128] = small_ref[...]


def fold_kernel(keep, crossed, mine, swap):
    z, _, _ = place()
    here = z % 2 == 0
    for i, (at, got) in enumerate(((0, 0), (3, 2))):
        for ref, j in ((mine, 0), (swap, 1)):
            row = jnp.where(here, crossed[got + j : got + j + 1, :], F32(-1.0))
            ref[i : i + 1, :] = jnp.maximum(keep[at + 4 * j : at + 4 * j + 1, :], row)


def merge_kernel(mine, other, small_ref, own, p1):
    own[...] = jnp.maximum(mine[0:1, :], other[0:1, :])
    row = jnp.maximum(mine[1:2, :], other[1:2, :])
    p1[0:8, :] = jnp.broadcast_to(row, (8, row.shape[1]))
    p1[8:16, 0:128] = small_ref[...]


def small_kernel(own, own_c, p0, c0, p2, c2, p3, c3, out_ref):
    z, k, _ = place()
    lanes = own.shape[0] - META
    dests, cap = META, lanes // META
    out_ref[...] = jnp.full(out_ref.shape, -1.0, F32)

    @pl.when(z == 1)
    def _():
        mine, others = (p0, own, p2, p3), (c0, own_c, c2, c3)
        meta = sum(p[lanes:, 0 : 3 * lanes].astype(F32) for p in mine + others)
        clus = meta[:, 0:lanes]
        order = meta[:, lanes : 2 * lanes] * DIGIT + meta[:, 2 * lanes :]
        clus_t, order_t = clus.T, order.T
        first = k == 0
        for j in range(dests):
            at = slice(j * cap, (j + 1) * cap)
            a = jnp.concatenate([p[at, :] for p in mine], axis=0)
            b = jnp.concatenate([p[at, :] for p in others], axis=0)
            slots = jnp.concatenate([jnp.where(first, a, b), jnp.where(first, b, a)], axis=0)
            s = lax.dot_general(slots, slots, NT, preferred_element_type=F32)
            allowed = (
                (clus_t[:, j : j + 1] == clus[j : j + 1, :])
                & (clus[j : j + 1, :] >= 0)
                & (order_t[:, j : j + 1] < order[j : j + 1, :])
            )
            out_ref[j : j + 1, :] = jnp.max(jnp.where(allowed, s, F32(-1.0)), axis=0, keepdims=True)


def final_kernel(inner, mine, small, g1, g2, g3, big_ref, small_ref):
    z, k, _ = place()

    def from_chip(when, ref):
        return jnp.where(when, ref[0:1, :], F32(-1.0))

    rows = (inner[...], mine[...], from_chip(z == 3, g1), from_chip(z == 1, g2), from_chip(z <= 1, g3))
    big_ref[...] = functools.reduce(jnp.maximum, rows)

    _, cap = small_ref.shape
    lanes = small.shape[1]
    near = jnp.where(z == 0, g2[8:16, 0:lanes], small[...])
    got = jnp.where(z == 2, g1[8:16, 0:lanes], jnp.where(z == 3, g3[8:16, 0:lanes], near))
    small_ref[...] = pltpu.roll(got, lanes - (k * (lanes // 2) + z * cap), 1)[:, 0:cap]


def line_body(big_emb, big_order, small_emb, small_clus, small_order):
    n, d = big_emb.shape
    _, dests, cap, _ = small_emb.shape
    chips = dests // 2
    lanes = dests * cap

    def move(value, to):
        pairs = []
        for z in range(chips):
            for k in range(2):
                for x in range(2):
                    t = to(z, k, x)
                    if t is not None:
                        pairs.append(((2 * z + k) * 2 + x, (2 * t[0] + t[1]) * 2 + t[2]))
        return lax.ppermute(value, BOTH, pairs)

    def hop(value, targets):
        return move(value, lambda z, k, x: (targets[z], k, x) if z in targets else None)

    def core(value):
        return move(value, lambda z, k, x: (z, 1 - k, x))

    def col(value):
        return move(value, lambda z, k, x: (z, k, 1 - x))

    def shape(rows, cols, kind=F32):
        return jax.ShapeDtypeStruct((rows, cols), kind)

    pair = 2 * n * n * d
    s_emb = small_emb.reshape(dests, cap, d)
    s_clus, s_ord = small_clus.reshape(dests, cap), small_order.reshape(dests, cap)
    block, part = shape(n + META, d, BF16), shape(n // 2 + META, d, BF16)
    digits = jnp.stack([big_order >> 8, big_order & (DIGIT - 1)]).astype(F32).astype(BF16)
    meta = jnp.pad(digits, ((0, META - 2), (0, d - n)))
    own, top, bot = call(prep_kernel, (block, part, part), big_emb, meta)
    a = hop(own, {1: 2})
    t = hop(own, {3: 2, 1: 0})
    x = col(own)
    c = core(own)

    s1, first = call(prep_small_kernel, (part, part), s_emb, s_clus, s_ord, top)
    s2 = hop(first, {0: 2, 2: 1})
    b2 = hop(bot, {0: 2})
    s0, s3 = hop(s1, {0: 1}), hop(s1, {3: 1})
    s1c = core(s1)
    xc, tc = core(x), core(t)
    d0 = move(x, lambda z, k, x: (2, 0, x) if (z, k) == (3, 0) else None)
    d1 = move(t, lambda z, k, x: (2, 1, 1 - x) if (z, k) == (2, 1) else None)
    dg = call(pick_kernel, block, d0, d1)
    dc = core(dg)

    plane = (own, c, x, xc, t)
    table = shape(TABLE, n)
    cols, inner = call(plane_kernel, (table, shape(1, n)), *plane, flops=8 * pair)
    s0c, s2c, s3c = core(s0), core(s2), core(s3)
    small = call(
        small_kernel,
        shape(8, lanes),
        s1, s1c, s0, s0c, s2, s2c, s3, s3c,
        flops=dests * 2 * lanes * lanes * d,
    )

    cols, b = call(left_b_kernel, (table, block), *plane, tc, s2, b2, cols, flops=6 * pair)
    cols = call(left_a_kernel, table, *plane, tc, a, cols, flops=6 * pair)
    crossed = call(cross_kernel, shape(4, n), cols)
    gx = col(crossed)
    pay = shape(16, n)
    keep, r2, r3 = call(late_kernel, (table, pay, pay), dg, dc, a, b, cols, small, flops=4 * pair)
    g3 = hop(r3, {2: 0, 0: 1, 1: 3})
    mine, swap = call(fold_kernel, (shape(2, n), shape(2, n)), keep, gx)
    got = core(swap)
    g2 = hop(r2, {2: 1, 1: 0})
    mine, r1 = call(merge_kernel, (shape(1, n), pay), mine, got, small)
    g1 = move(r1, lambda z, k, x: {2: (3, k, 1 - x), 1: (2, k, x)}.get(z))
    big, sm = call(final_kernel, (shape(1, n), shape(dests, cap)), inner, mine, small, g1, g2, g3)
    return big.reshape(n), sm.reshape(1, dests, cap)


def fits(mesh, n, dests, cap):
    rows, cols = mesh.shape["rows"], mesh.shape["cols"]
    return rows == 8 and cols == 2 and dests == META and n == 2 * dests * cap and n == DIGIT


def solution(mesh):
    placed = (
        P(("groups", "rows", "cols"), None),
        P(("groups", "rows", "cols")),
        P(("groups", "rows", "cols"), None, None, None),
        P(("groups", "rows", "cols"), None, None),
        P(("groups", "rows", "cols"), None, None),
    )
    parts = mesh.size

    def over(local):
        return jax.shard_map(
            local,
            mesh=mesh,
            in_specs=placed,
            out_specs=(P(("groups", "rows", "cols")), P(("groups", "rows", "cols"), None, None)),
            check_vma=False,
        )

    line = over(line_body)

    def step(big_emb, big_order, small_emb, small_clus, small_order):
        args = (big_emb, big_order, small_emb, small_clus, small_order)
        ok = fits(mesh, big_emb.shape[0] // parts, small_emb.shape[1], small_emb.shape[2])
        return line(*args) if ok else over(local_any)(*args)

    return step
```

```python
import functools

import jax
import jax.numpy as jnp
from jax import lax
from jax.experimental import pallas as pl
from jax.experimental.pallas import tpu as pltpu
from jax.sharding import PartitionSpec as P


F32, BF16 = jnp.float32, jnp.bfloat16
BOTH = ("rows", "cols")
NT = (((1,), (1,)), ((), ()))
NN = (((1,), (0,)), ((), ()))
META = 8
DIGIT = 256


def normalize(values):
    floats = values.astype(F32)
    squares = jnp.sum(floats * floats, axis=-1, keepdims=True)
    return (floats * lax.rsqrt(squares + 1e-06)).astype(BF16)


def best_over(row_emb, row_ord, col_emb, col_ord):
    total_rows = row_emb.shape[0]
    height = 512 if total_rows % 512 == 0 else total_rows

    def one_block(block_at):
        rows_here = lax.dynamic_slice_in_dim(row_emb, block_at * height, height, 0)
        ord_here = lax.dynamic_slice_in_dim(row_ord, block_at * height, height, 0)
        scores = lax.dot_general(rows_here, col_emb, NT, preferred_element_type=F32)
        allowed = col_ord[None, :] < ord_here[:, None]
        return jnp.max(jnp.where(allowed, scores, F32(-1.0)), axis=1)

    blocks = lax.map(one_block, jnp.arange(total_rows // height, dtype=jnp.int32))
    return jnp.maximum(blocks.reshape(total_rows), F32(-1.0))


def cluster_best(slots, clusters, orders):
    scores = lax.dot_general(slots, slots, NT, preferred_element_type=F32)
    allowed = (
        (clusters[None, :] == clusters[:, None])
        & (clusters[:, None] >= 0)
        & (orders[None, :] < orders[:, None])
    )
    return jnp.max(jnp.where(allowed, scores, F32(-1.0)), axis=1)


def local_any(big_emb, big_order, small_emb, small_clus, small_order):
    own_rows = big_emb.shape[0]
    big_unit = normalize(big_emb)
    small_unit = normalize(small_emb)
    sent_emb, sent_clus, sent_ord = (
        lax.all_to_all(v, "rows", split_axis=1, concat_axis=1, tiled=True)
        for v in (small_unit, small_clus, small_order)
    )
    depth = sent_emb.shape[1] * sent_emb.shape[2]
    slot_best = cluster_best(
        sent_emb.reshape(depth, sent_emb.shape[3]),
        sent_clus.reshape(depth),
        sent_ord.reshape(depth),
    )
    slot_best = slot_best.reshape(sent_clus.shape)
    partial_value = best_over(
        lax.all_gather(big_unit, "cols", axis=0, tiled=True),
        lax.all_gather(big_order, "cols", axis=0, tiled=True),
        lax.all_gather(big_unit, "rows", axis=0, tiled=True),
        lax.all_gather(big_order, "rows", axis=0, tiled=True),
    )
    merged = lax.pmax(partial_value, "cols")
    big_best = lax.dynamic_slice_in_dim(merged, lax.axis_index("cols") * own_rows, own_rows, 0)
    small_best = lax.all_to_all(slot_best, "rows", split_axis=1, concat_axis=1, tiled=True)
    return (big_best, small_best)


def call(kernel, outs, *args, flops=0, scratch=(), space=pltpu.VMEM):
    moved = sum(a.size * a.dtype.itemsize for a in args)
    return pl.pallas_call(
        kernel,
        out_shape=outs,
        in_specs=[pl.BlockSpec(memory_space=space)] * len(args),
        out_specs=jax.tree.map(lambda _: pl.BlockSpec(memory_space=pltpu.VMEM), outs),
        scratch_shapes=list(scratch),
        compiler_params=pltpu.CompilerParams(vmem_limit_bytes=10 << 20),
        cost_estimate=pl.CostEstimate(flops=flops, bytes_accessed=moved, transcendentals=0),
    )(*args)


def place():
    r = lax.axis_index("rows")
    return r // 2, r % 2, lax.axis_index("cols")


def unit(values):
    floats = values.astype(F32)
    squares = jnp.sum(floats * floats, axis=-1, keepdims=True)
    return (floats * lax.rsqrt(squares + 1e-06)).astype(BF16)


def prep_small_kernel(s_ref, clus_ref, ord_ref, out):
    dests, cap, d = s_ref.shape
    z, k, _ = place()
    lanes = dests * cap
    slot = lax.broadcasted_iota(jnp.int32, (cap, lanes), 0)
    lane = lax.broadcasted_iota(jnp.int32, (cap, lanes), 1)
    spread = jnp.where(lane == slot + k * (lanes // 2) + z * cap, 1.0, 0.0).astype(BF16)
    for j in range(dests):
        out[j * cap : (j + 1) * cap, :] = unit(s_ref[j])
    orders = ord_ref[...]
    for at, digits in enumerate((clus_ref[...], orders >> 8, orders & (DIGIT - 1))):
        rows = lax.dot_general(digits.astype(F32).astype(BF16), spread, NN, preferred_element_type=F32)
        out[lanes:, at * lanes : (at + 1) * lanes] = rows.astype(BF16)
    out[lanes:, 3 * lanes :] = jnp.zeros((META, d - 3 * lanes), BF16)


def prep_kernel(x_ref, meta_ref, own):
    n, _ = x_ref.shape
    own[0:n, :] = unit(x_ref[...])
    own[n:, :] = meta_ref[...]


def order_row(ref):
    n = ref.shape[0] - META
    digits = ref[n:, 0:n].astype(F32)
    return digits[0:1] * DIGIT + digits[1:2]


def order_col(ref):
    row = order_row(ref)
    n = row.shape[1]
    return jnp.broadcast_to(row, (128, n)).T[:, 0:1]


def scores_of(y_ref, x_ref):
    n = x_ref.shape[0] - META
    return lax.dot_general(y_ref[0:n, :], x_ref[0:n, :], NT, preferred_element_type=F32)


def sweep(x_ref, y_refs, cols):
    own = order_col(x_ref)
    best = None
    for at, y in y_refs:
        s = scores_of(x_ref, y)
        later = order_row(y) < own
        mine = jnp.where(later, s, F32(-1.0))
        best = mine if best is None else jnp.maximum(best, mine)
        other = jnp.max(jnp.where(later, F32(-1.0), s), axis=0, keepdims=True)
        cols[at : at + 1, :] = jnp.maximum(cols[at : at + 1, :], other)
    n = best.shape[1]
    folded = functools.reduce(jnp.maximum, [best[:, j : j + 128] for j in range(0, n, 128)])
    return jnp.max(folded.T, axis=0, keepdims=True)


PLANE = (0, 4, 1, 5)
RIGHT = (2, 6, 3, 7)
ROW_T, ROW_A, ROW_B = 8, 9, 10
TABLE = 16


def plane_kernel(own, c, x, xc, t, cols_ref, inner_ref):
    z, _, _ = place()
    cols_ref[...] = jnp.full(cols_ref.shape, -1.0, F32)
    mine = order_row(own)
    best = None
    for y in (own, c, x, xc):
        s = jnp.where(order_col(y) < mine, scores_of(y, own), F32(-1.0))
        best = s if best is None else jnp.maximum(best, s)
    inner_ref[...] = jnp.max(best, axis=0, keepdims=True)

    @pl.when(z % 2 == 0)
    def _():
        cols_ref[ROW_T : ROW_T + 1, :] = sweep(t, list(zip(PLANE, (own, c, x, xc))), cols_ref)


def left_kernel(result, own, c, x, xc, t, tc, block, cols_ref, out_ref):
    z, _, _ = place()
    out_ref[...] = cols_ref[...]

    @pl.when(z == 2)
    def _():
        met = list(zip(PLANE, (own, c, x, xc))) + list(zip(RIGHT, (t, tc)))
        out_ref[result : result + 1, :] = sweep(block, met, out_ref)


def pick_kernel(first, second, out):
    _, k, _ = place()
    for core, ref in enumerate((first, second)):

        @pl.when(k == core)
        def _(ref=ref):
            out[...] = ref[...]


def cross_kernel(cols, out):
    z, _, _ = place()
    for i, at in enumerate((1, 5, 2, 6)):
        out[i : i + 1, :] = cols[at : at + 1, :]

    @pl.when(z == 2)
    def _():
        out[2:3, :] = jnp.maximum(cols[2:3, :], cols[ROW_T : ROW_T + 1, :])


def late_kernel(d, dc, a, b, cols_ref, small_ref, keep, p2, p3):
    z, _, _ = place()
    keep[...] = cols_ref[...]

    @pl.when(z == 2)
    def _():
        far = list(zip(RIGHT[2:], (d, dc)))
        for block, at in ((a, ROW_A), (b, ROW_B)):
            row = sweep(block, far, keep)
            keep[at : at + 1, :] = jnp.maximum(keep[at : at + 1, :], row)

    first = jnp.where(z == 0, keep[ROW_T : ROW_T + 1, :], keep[ROW_B : ROW_B + 1, :])
    for ref, row in ((p2, keep[ROW_A : ROW_A + 1, :]), (p3, first)):
        ref[0:8, :] = jnp.broadcast_to(row, (8, row.shape[1]))
        ref[8:16, 0:128] = small_ref[...]


def fold_kernel(keep, crossed, mine, swap):
    z, _, _ = place()
    here = z % 2 == 0
    for i, (at, got) in enumerate(((0, 0), (3, 2))):
        for ref, j in ((mine, 0), (swap, 1)):
            row = jnp.where(here, crossed[got + j : got + j + 1, :], F32(-1.0))
            ref[i : i + 1, :] = jnp.maximum(keep[at + 4 * j : at + 4 * j + 1, :], row)


def merge_kernel(mine, other, small_ref, own, p1):
    own[...] = jnp.maximum(mine[0:1, :], other[0:1, :])
    row = jnp.maximum(mine[1:2, :], other[1:2, :])
    p1[0:8, :] = jnp.broadcast_to(row, (8, row.shape[1]))
    p1[8:16, 0:128] = small_ref[...]


def small_kernel(own, own_c, p0, c0, p2, c2, p3, c3, out_ref):
    z, k, _ = place()
    lanes = own.shape[0] - META
    dests, cap = META, lanes // META
    out_ref[...] = jnp.full(out_ref.shape, -1.0, F32)

    @pl.when(z == 1)
    def _():
        mine, others = (p0, own, p2, p3), (c0, own_c, c2, c3)
        meta = sum(p[lanes:, 0 : 3 * lanes].astype(F32) for p in mine + others)
        clus = meta[:, 0:lanes]
        order = meta[:, lanes : 2 * lanes] * DIGIT + meta[:, 2 * lanes :]
        clus_t, order_t = clus.T, order.T
        first = k == 0
        for j in range(dests):
            at = slice(j * cap, (j + 1) * cap)
            a = jnp.concatenate([p[at, :] for p in mine], axis=0)
            b = jnp.concatenate([p[at, :] for p in others], axis=0)
            slots = jnp.concatenate([jnp.where(first, a, b), jnp.where(first, b, a)], axis=0)
            s = lax.dot_general(slots, slots, NT, preferred_element_type=F32)
            allowed = (
                (clus_t[:, j : j + 1] == clus[j : j + 1, :])
                & (clus[j : j + 1, :] >= 0)
                & (order_t[:, j : j + 1] < order[j : j + 1, :])
            )
            out_ref[j : j + 1, :] = jnp.max(jnp.where(allowed, s, F32(-1.0)), axis=0, keepdims=True)


def final_kernel(inner, mine, small, g1, g2, g3, big_ref, small_ref):
    z, k, _ = place()

    def from_chip(when, ref):
        return jnp.where(when, ref[0:1, :], F32(-1.0))

    rows = (inner[...], mine[...], from_chip(z == 3, g1), from_chip(z == 1, g2), from_chip(z <= 1, g3))
    big_ref[...] = functools.reduce(jnp.maximum, rows)

    _, cap = small_ref.shape
    lanes = small.shape[1]
    near = jnp.where(z == 0, g2[8:16, 0:lanes], small[...])
    got = jnp.where(z == 2, g1[8:16, 0:lanes], jnp.where(z == 3, g3[8:16, 0:lanes], near))
    small_ref[...] = pltpu.roll(got, lanes - (k * (lanes // 2) + z * cap), 1)[:, 0:cap]


def line_body(big_emb, big_order, small_emb, small_clus, small_order):
    n, d = big_emb.shape
    _, dests, cap, _ = small_emb.shape
    chips = dests // 2
    lanes = dests * cap

    def move(value, to):
        pairs = []
        for z in range(chips):
            for k in range(2):
                for x in range(2):
                    t = to(z, k, x)
                    if t is not None:
                        pairs.append(((2 * z + k) * 2 + x, (2 * t[0] + t[1]) * 2 + t[2]))
        return lax.ppermute(value, BOTH, pairs)

    def hop(value, targets):
        return move(value, lambda z, k, x: (targets[z], k, x) if z in targets else None)

    def core(value):
        return move(value, lambda z, k, x: (z, 1 - k, x))

    def col(value):
        return move(value, lambda z, k, x: (z, k, 1 - x))

    def shape(rows, cols, kind=F32):
        return jax.ShapeDtypeStruct((rows, cols), kind)

    pair = 2 * n * n * d
    s_emb = small_emb.reshape(dests, cap, d)
    s_clus, s_ord = small_clus.reshape(dests, cap), small_order.reshape(dests, cap)
    block, part = shape(n + META, d, BF16), shape(n // 2 + META, d, BF16)
    digits = jnp.stack([big_order >> 8, big_order & (DIGIT - 1)]).astype(F32).astype(BF16)
    meta = jnp.pad(digits, ((0, META - 2), (0, d - n)))
    own = call(prep_kernel, block, big_emb, meta)
    a = hop(own, {1: 2})
    t = hop(own, {3: 2, 1: 0})
    x = col(own)
    b = hop(own, {0: 2})
    c = core(own)

    s1 = call(prep_small_kernel, part, s_emb, s_clus, s_ord)
    s0, s3, s2 = hop(s1, {0: 1}), hop(s1, {3: 1}), hop(s1, {2: 1})
    s1c = core(s1)
    xc, tc = core(x), core(t)
    d0 = move(x, lambda z, k, x: (2, 0, x) if (z, k) == (3, 0) else None)
    d1 = move(t, lambda z, k, x: (2, 1, 1 - x) if (z, k) == (2, 1) else None)
    dg = call(pick_kernel, block, d0, d1)
    dc = core(dg)

    plane = (own, c, x, xc, t)
    table = shape(TABLE, n)
    cols, inner = call(plane_kernel, (table, shape(1, n)), *plane, flops=8 * pair)
    s0c, s2c, s3c = core(s0), core(s2), core(s3)
    small = call(
        small_kernel,
        shape(8, lanes),
        s1, s1c, s0, s0c, s2, s2c, s3, s3c,
        flops=dests * 2 * lanes * lanes * d,
    )

    for row, left in ((ROW_B, b), (ROW_A, a)):
        cols = call(functools.partial(left_kernel, row), table, *plane, tc, left, cols, flops=6 * pair)
    crossed = call(cross_kernel, shape(4, n), cols)
    gx = col(crossed)
    pay = shape(16, n)
    keep, r2, r3 = call(late_kernel, (table, pay, pay), dg, dc, a, b, cols, small, flops=4 * pair)
    g3 = hop(r3, {2: 0, 0: 1, 1: 3})
    mine, swap = call(fold_kernel, (shape(2, n), shape(2, n)), keep, gx)
    got = core(swap)
    g2 = hop(r2, {2: 1, 1: 0})
    mine, r1 = call(merge_kernel, (shape(1, n), pay), mine, got, small)
    g1 = move(r1, lambda z, k, x: {2: (3, k, 1 - x), 1: (2, k, x)}.get(z))
    big, sm = call(final_kernel, (shape(1, n), shape(dests, cap)), inner, mine, small, g1, g2, g3)
    return big.reshape(n), sm.reshape(1, dests, cap)


def fits(mesh, n, dests, cap):
    rows, cols = mesh.shape["rows"], mesh.shape["cols"]
    return rows == 8 and cols == 2 and dests == META and n == 2 * dests * cap and n == DIGIT


def solution(mesh):
    placed = (
        P(("groups", "rows", "cols"), None),
        P(("groups", "rows", "cols")),
        P(("groups", "rows", "cols"), None, None, None),
        P(("groups", "rows", "cols"), None, None),
        P(("groups", "rows", "cols"), None, None),
    )
    parts = mesh.size

    def over(local):
        return jax.shard_map(
            local,
            mesh=mesh,
            in_specs=placed,
            out_specs=(P(("groups", "rows", "cols")), P(("groups", "rows", "cols"), None, None)),
            check_vma=False,
        )

    line = over(line_body)

    def step(big_emb, big_order, small_emb, small_clus, small_order):
        args = (big_emb, big_order, small_emb, small_clus, small_order)
        ok = fits(mesh, big_emb.shape[0] // parts, small_emb.shape[1], small_emb.shape[2])
        return line(*args) if ok else over(local_any)(*args)

    return step
```
